128 devices in a mesh: lag: 8 (over y, core), col: 16 (over z, x).
Axes of the slice: x: 4, y: 4, z: 4, core: 2. Of those that a mesh axis runs over, the one named last changes fastest.
Arguments:
- lag_matrices: float32 [128, 2048, 2048], P('lag', None, 'col'), may hold values from -0.03125 to 0.03125
- history: float32 [128, 2048, 256], P('lag', 'col'), may hold values from -6 to 6
- excitation: float32 [4, 2048, 256], P(None, 'col'), may hold values from -6 to 6
Outputs:
- densities: float32 [4, 2048, 256], P(None, 'col')
The draws below stay inside these ranges and needn't reach their ends.
All inputs are finite; a program needn't handle non-finite values.
Results may differ from the reference program's by a relative error of at most 0.0001.
Values sent between devices are 32-bit elements; how exact they have to be, the bound alone decides.
A program may use at most 64 MiB of HBM per device.

```python
import jax
import jax.numpy as jnp
from jax import lax

U = 2048
R = 256
STEPS = 4
LAGS = 128


def with_spikes(drawn, stream_key, source, target, shards_of, factor):
    def block_of(dim):
        return (jnp.arange(drawn.shape[dim]) // (drawn.shape[dim] // shards_of)).reshape((-1,) + (1,) * (drawn.ndim - 1 - dim))

    one_side = jax.random.permutation(stream_key, shards_of)[block_of(target)]
    far = (block_of(target) + shards_of // 2) % shards_of
    return jnp.where((block_of(source) == one_side) | (block_of(source) == far), factor * drawn, drawn)


def shard_levels(own_key, extent, pieces, low, largest):
    factor_of, own = 1.0, jax.random.fold_in(own_key, 6)
    for dim, parts in pieces:
        heights = jnp.exp(jax.random.uniform(jax.random.fold_in(own, dim), (parts,), jnp.float32, low / len(pieces), largest / len(pieces)))
        factor_of = factor_of * jnp.repeat(heights, extent[dim] // parts).reshape([-1 if axis == dim else 1 for axis in range(len(extent))])
    return factor_of


def normal_values(rng, shape, scale, bound, cuts=(), held_as=jnp.bfloat16):
    gain = shard_levels(rng, shape, cuts, -0.22, 0.18) if cuts else 1.0
    result = jax.random.normal(rng, shape, jnp.float32) * scale * gain
    return jnp.minimum(jnp.maximum(result, -bound), bound).astype(held_as)


def gaussian_with(stream_key, extent, scale, most, cuts, heavy, kind=jnp.bfloat16):
    result = scale * jax.random.normal(stream_key, extent, jnp.float32)
    if cuts:
        result = result * shard_levels(stream_key, extent, cuts, -0.22, 0.18)
    return jnp.clip(with_spikes(result, jax.random.fold_in(stream_key, 3), *heavy), -most, most).astype(kind)


def setup_inputs(seed: int = 0) -> dict:
    seeds = jax.random.split(jax.random.key(seed), 4)
    return {
        "lag_matrices": gaussian_with(seeds[0], (LAGS, U, U), (40 * U) ** -0.5, 0.03125, ((0, 8), (2, 16)), (2, 1, 16, 2.0), jnp.float32),
        "history": normal_values(seeds[1], (LAGS, U, R), 1.0, 6.0, ((0, 8), (1, 16)), jnp.float32),
        "excitation": normal_values(seeds[2], (STEPS, U, R), 1.0, 6.0, ((1, 16),), jnp.float32),
    }


def reference(lag_matrices, history, excitation):
    densities = []
    for moment in range(STEPS):
        if moment > 0:
            recent = jnp.stack([densities[moment - 1 - offset] for offset in range(moment)])
            stacked = jnp.concatenate([recent, history[:LAGS - moment]], axis=0)
        else:
            stacked = history
        total = jnp.einsum("kab,kbr->ar", lag_matrices, stacked, precision=lax.Precision.HIGHEST)
        densities.append(excitation[moment] - total)
    return jnp.stack(densities)
```

```python
import jax
import jax.numpy as jnp
from jax import lax
from jax.experimental import pallas as pl
from jax.experimental.pallas import tpu as pltpu
from jax.sharding import PartitionSpec as P

MESH = pl.DeviceIdType.MESH
bf, f32 = jnp.bfloat16, jnp.float32

RING = 4
SLOTS = 8
SUB = 3
LAG_EXCH, LAG_ONE, LAG_TWO, LAG_THREE = 2, 3, 3, 3
LAG_GATHER, LAG_SCATTER = 3, 5


def halves(value):
    high = value.astype(bf)
    return high, (value - high.astype(f32)).astype(bf)


def dot(a, b):
    return jnp.dot(a, b, preferred_element_type=f32)


def kernel(
    a_ref, h_ref, e_ref, o_ref,
    mats, ext, xh, xl, both, first, part, swap,
    in1, sum1, in2, sum2, in3, total,
    near, near_b, terms, in_t, new, new_b, exc,
    s_mat, s_loc, s_carry, r_carry, s_near, r_near, s_fwd, r_fwd,
    s_swap, r_swap, s1, r1, s2, r2, s3, r3, s_t, r_t, s_g, r_g, s_o, r_o,
):
    lag, col = lax.axis_index("lag"), lax.axis_index("col")
    y, k = lag // 2, lag % 2
    z, x = col // RING, col % RING
    pos = {"x": x, "y": y, "z": z}
    other = 1 - k

    def device(**moved):
        at = {**pos, "k": k, **moved}
        return (at["y"] * 2 + at["k"], at["z"] * RING + at["x"])

    def turned(axis, steps):
        return lax.rem(pos[axis] + steps, RING)

    def send(src, dst, s_sem, r_sem, target):
        pltpu.make_async_remote_copy(
            src_ref=src, dst_ref=dst, send_sem=s_sem, recv_sem=r_sem,
            device_id=target, device_id_type=MESH,
        ).start()

    def await_bytes(ref, sem):
        pltpu.make_async_copy(ref, ref, sem).wait()

    load_h = pltpu.make_async_copy(h_ref, ext.at[pl.ds(3, 16)], s_loc.at[0])
    load_h.start()
    load_a = [
        pltpu.make_async_copy(a_ref.at[:, :, :, pl.ds(8 * t, 8)], mats.at[t], s_mat.at[t])
        for t in range(4)
    ]
    load_a[0].start()
    load_e = pltpu.make_async_copy(e_ref, exc, s_loc.at[1])
    load_e.start()
    for t in range(1, 4):
        load_a[t].start()

    barrier = pltpu.get_barrier_semaphore()
    cross = (lax.rem(y + jnp.where(k == 1, 1, RING - 1), RING) * 2 + other, col)
    peers = [device(k=other), cross]
    peers += [device(y=turned("y", d)) for d in range(1, RING)]
    peers += [
        device(z=turned("z", dz), x=turned("x", dx))
        for dz in range(RING) for dx in range(RING) if dz or dx
    ]
    for peer in peers:
        pl.semaphore_signal(barrier, inc=1, device_id=peer, device_id_type=MESH)

    @pl.when(lag == 0)
    def _():
        ext[0:3] = jnp.zeros((3, 128, 256), f32)

    load_h.wait()

    def set_block(kind, u):
        base = ext[1 + 2 * u]
        value = (base, ext[2 + 2 * u] - base, ext[2 * u] - base)[kind]
        rows = pl.ds(u * 128, 128)
        xh[kind, rows], xl[kind, rows] = halves(value)

    pl.semaphore_wait(barrier, len(peers))

    @pl.when(lag < 7)
    def _():
        after = (lag + 1, col)
        send(h_ref.at[15], ext.at[2], s_carry.at[0], r_carry.at[0], after)
        send(h_ref.at[pl.ds(13, 2)], ext.at[pl.ds(0, 2)], s_carry.at[1], r_carry.at[1], after)

    @pl.when(lag == 0)
    def _():
        pltpu.make_async_copy(a_ref.at[pl.ds(0, 3), :, 0], near, s_loc.at[2]).start()
        for j in range(3):
            for d in (1, 3, 2):
                send(a_ref.at[j, :, d], near.at[j], s_near, r_near, device(y=d))

    for u in range(2, 9):
        for kind in range(3):
            set_block(kind, u)
    for kind in range(2):
        set_block(kind, 1)

    events = {}

    def at(time, act):
        events.setdefault(time, []).append(act)

    def swap_send(s, n):
        send(part.at[s, n, other], swap.at[s, n], s_swap, r_swap.at[s, n], device(k=other))

    orders = (("x", "y", "z"), ("y", "z", "x"), ("z", "x", "y"))
    MEMORY = ("z", "x", "y")

    def block(ref, lead, axes, axis, index):
        return ref.at[(*lead, *(index if name == axis else slice(None) for name in axes))]

    def exchange(s, n):
        await_bytes(swap.at[s, n], r_swap.at[s, n])
        part[s, n, k] += swap[s, n]
        axis = orders[(2 * s + n) % 3][0]
        for d in (2, 1, 3):
            to = turned(axis, d)
            send(
                block(part, (s, n, k), MEMORY, axis, to), in1.at[s, n, d - 1],
                s1, r1.at[s, n], device(**{axis: to}),
            )

    def one(s, n):
        order = orders[(2 * s + n) % 3]
        left = tuple(name for name in MEMORY if name != order[0])
        await_bytes(in1.at[s, n], r1.at[s, n])
        mine = block(part, (s, n, k), MEMORY, order[0], pos[order[0]])[...]
        sum1[s, n] = (mine + in1[s, n, 0]) + (in1[s, n, 1] + in1[s, n, 2])
        for d in (2, 1, 3):
            to = turned(order[1], d)
            send(
                block(sum1, (s, n), left, order[1], to), in2.at[s, n, d - 1],
                s2, r2.at[s, n], device(**{order[1]: to}),
            )

    def two(s, n):
        order = orders[(2 * s + n) % 3]
        left = tuple(name for name in MEMORY if name != order[0])
        await_bytes(in2.at[s, n], r2.at[s, n])
        mine = block(sum1, (s, n), left, order[1], pos[order[1]])[...]
        sum2[s, n] = (mine + in2[s, n, 0]) + (in2[s, n, 1] + in2[s, n, 2])
        for d in (2, 1, 3):
            to = turned(order[2], d)
            send(
                sum2.at[s, n, to], in3.at[s, n, d - 1],
                s3, r3.at[s, n], device(**{order[2]: to}),
            )

    def three(s, n):
        order = orders[(2 * s + n) % 3]
        await_bytes(in3.at[s, n], r3.at[s, n])
        mine = sum2[s, n, pos[order[2]]]
        total[2 * (s // 4) + n, s % 4] = (mine + in3[s, n, 0]) + (in3[s, n, 1] + in3[s, n, 2])

    for s in range(SLOTS):
        for n in range(2):
            time = SUB * s + 1 + n
            at(time, lambda s=s, n=n: swap_send(s, n))
            at(time + LAG_EXCH, lambda s=s, n=n: exchange(s, n))
            at(time + LAG_EXCH + LAG_ONE, lambda s=s, n=n: one(s, n))
            at(time + LAG_EXCH + LAG_ONE + LAG_TWO, lambda s=s, n=n: two(s, n))
            at(time + LAG_EXCH + LAG_ONE + LAG_TWO + LAG_THREE, lambda s=s, n=n: three(s, n))

    def near_pass():
        @pl.when(k == 0)
        def _():
            @pl.when(y == 0)
            def _():
                pltpu.make_async_copy(a_ref.at[pl.ds(0, 3), :, 0], near, s_loc.at[2]).wait()

            @pl.when(y > 0)
            def _():
                await_bytes(near, r_near)

            send(near, near, s_fwd, r_fwd, device(k=1))

        @pl.when(k == 1)
        def _():
            await_bytes(near, r_fwd)

    def near_split():
        for j in range(3):
            high, low = halves(near[j].reshape(512, 128))
            near_b[j, :, 0:128] = high
            near_b[j, :, 128:256] = high
            near_b[j, :, 256:384] = low

    def finish(n):
        value = exc[n, pl.ds(y * 32, 32), pl.ds(pl.multiple_of(k * 128, 128), 128)] - total[n].reshape(32, 128)
        if n > 0:
            await_bytes(in_t.at[n - 1], r_t.at[n - 1])
            value = value - (terms[n - 1, z, x] + in_t[n - 1].sum(axis=0))
        new[n, y] = value
        for d in (2, 1, 3):
            send(new.at[n, y], new.at[n, y], s_g.at[n], r_g.at[n], device(y=turned("y", d)))

    def gathered(n):
        await_bytes(new.at[n, pl.ds(0, 3)], r_g.at[n])
        own = pl.ds(pl.multiple_of(k * 128, 128), 128)
        if n < 3:
            value = new[n].reshape(128, 128)
            high, low = halves(value)
            new_b[n, 0:128] = high
            new_b[n, 128:256] = low
            new_b[n, 256:384] = high
            product = dot(near_b[0], new_b[n])
            if n > 0:
                product = product + terms[n].reshape(512, 128)
            terms[n] = product.reshape(RING, RING, 32, 128)
            for dz in (2, 1, 3, 0):
                for dx in (2, 1, 3, 0):
                    if dz or dx:
                        tz, tx = turned("z", dz), turned("x", dx)
                        send(
                            terms.at[n, tz, tx], in_t.at[n, RING * dz + dx - 1],
                            s_t.at[n], r_t.at[n], device(z=tz, x=tx),
                        )
        o_ref[n, :, own] = new[n].reshape(128, 128)
        send(o_ref.at[n, :, own], o_ref.at[n, :, own], s_o.at[n], r_o.at[n], device(k=other))
        if n < 2:
            for m in range(n + 1, 3):
                product = dot(near_b[m - n], new_b[n])
                if n > 0:
                    product = product + terms[m].reshape(512, 128)
                terms[m] = product.reshape(RING, RING, 32, 128)

    at(11, near_pass)
    at(14, near_split)
    time = SUB * 3 + 1 + LAG_EXCH + LAG_ONE + LAG_TWO + LAG_THREE
    for n in range(4):
        at(time, lambda n=n: finish(n))
        time += LAG_GATHER
        at(time, lambda n=n: gathered(n))
        time += LAG_SCATTER

    def build(t):
        def rows_of(i, carry):
            for u in range(8):
                columns = pl.ds(u * 128, 128)
                even = mats[t, 2 * u, i].reshape(32, 128)
                odd = mats[t, 2 * u + 1, i].reshape(32, 128)
                top = pl.ds(pl.multiple_of(i * 32, 32), 32)
                low = pl.ds(pl.multiple_of(512 + i * 32, 32), 32)
                both[0, top, columns], both[0, low, columns] = halves(even + odd)
                both[1, top, columns], both[1, low, columns] = halves(odd)
                both[2, top, columns], both[2, low, columns] = halves(even)
            return carry

        lax.fori_loop(0, 16, rows_of, 0)

    def product(kind, pair):
        depth = pl.ds((1 - pair) * 128, 1024)
        stacked = dot(both[kind], xh[kind, depth])
        return stacked[:512] + stacked[512:] + dot(both[kind, 0:512], xl[kind, depth])

    def store(s, n, value):
        for half in range(2):
            part[s, n, half] = value[:, half * 128 : half * 128 + 128].reshape(RING, RING, RING, 8, 128)

    def run(time):
        for act in events.pop(time, []):
            act()

    for s in range(SLOTS):
        pair, t = s // 4, s % 4
        if pair == 0:
            load_a[t].wait()
        if s == 3:
            load_e.wait()
        build(t)
        first[...] = product(0, pair)
        run(SUB * s)
        store(s, 0, first[...] + product(1, pair))
        run(SUB * s + 1)
        if s == 0:
            @pl.when(lag > 0)
            def _():
                await_bytes(ext.at[2], r_carry.at[0])
            set_block(2, 1)
        if s == 4:
            pass
        store(s, 1, first[...] + product(2, pair))
        run(SUB * s + 2)
        if s == 2:
            @pl.when(lag > 0)
            def _():
                await_bytes(ext.at[pl.ds(0, 2)], r_carry.at[1])
            for kind in range(3):
                set_block(kind, 0)

    for time in sorted(events):
        run(time)

    for n in range(4):
        await_bytes(o_ref.at[n, :, pl.ds(0, 128)], r_o.at[n])
        await_bytes(o_ref.at[n, :, pl.ds(0, 128)], s_o.at[n])
        await_bytes(new.at[n, pl.ds(0, 3)], s_g.at[n])
    for n in range(3):
        await_bytes(in_t.at[n], s_t.at[n])
    await_bytes(swap, s_swap)
    await_bytes(in1, s1)
    await_bytes(in2, s2)
    await_bytes(in3, s3)

    @pl.when(lag < 7)
    def _():
        await_bytes(ext.at[2], s_carry.at[0])
        await_bytes(ext.at[pl.ds(0, 2)], s_carry.at[1])

    @pl.when(lag == 0)
    def _():
        for _i in range(3):
            await_bytes(near, s_near)

    @pl.when(k == 0)
    def _():
        await_bytes(near, s_fwd)


def local(lag_matrices, history, excitation):
    DMA = pltpu.SemaphoreType.DMA
    return pl.pallas_call(
        kernel,
        out_shape=jax.ShapeDtypeStruct((4, 128, 256), f32),
        in_specs=[pl.BlockSpec(memory_space=pl.ANY)] * 3,
        out_specs=pl.BlockSpec(memory_space=pltpu.VMEM),
        scratch_shapes=[
            pltpu.VMEM((4, 16, 16, 4, 8, 128), f32),
            pltpu.VMEM((19, 128, 256), f32),
            pltpu.VMEM((3, 1152, 256), bf),
            pltpu.VMEM((3, 1152, 256), bf),
            pltpu.VMEM((3, 1024, 1024), bf),
            pltpu.VMEM((512, 256), f32),
            pltpu.VMEM((SLOTS, 2, 2, 4, 4, 4, 8, 128), f32),
            pltpu.VMEM((SLOTS, 2, 4, 4, 4, 8, 128), f32),
            pltpu.VMEM((SLOTS, 2, 3, 4, 4, 8, 128), f32),
            pltpu.VMEM((SLOTS, 2, 4, 4, 8, 128), f32),
            pltpu.VMEM((SLOTS, 2, 3, 4, 8, 128), f32),
            pltpu.VMEM((SLOTS, 2, 4, 8, 128), f32),
            pltpu.VMEM((SLOTS, 2, 3, 8, 128), f32),
            pltpu.VMEM((4, 4, 8, 128), f32),
            pltpu.VMEM((3, 16, 32, 128), f32),
            pltpu.VMEM((3, 512, 384), bf),
            pltpu.VMEM((3, 4, 4, 32, 128), f32),
            pltpu.VMEM((3, 15, 32, 128), f32),
            pltpu.VMEM((4, 4, 32, 128), f32),
            pltpu.VMEM((3, 384, 128), bf),
            pltpu.VMEM((4, 128, 256), f32),
            DMA((4,)), DMA((3,)), DMA((2,)), DMA((2,)), DMA, DMA, DMA, DMA,
            DMA, DMA((SLOTS, 2)), DMA, DMA((SLOTS, 2)), DMA, DMA((SLOTS, 2)), DMA, DMA((SLOTS, 2)),
            DMA((3,)), DMA((3,)), DMA((4,)), DMA((4,)), DMA((4,)), DMA((4,)),
        ],
        compiler_params=pltpu.CompilerParams(
            collective_id=0, has_side_effects=True, vmem_limit_bytes=66_000_000
        ),
    )(lag_matrices.reshape(16, 16, 4, 32, 128), history, excitation)


def solution(mesh):
    return jax.shard_map(
        local,
        mesh=mesh,
        in_specs=(P("lag", None, "col"), P("lag", "col", None), P(None, "col", None)),
        out_specs=P(None, "col", None),
        check_vma=False,
    )
```

```python
import jax
import jax.numpy as jnp
from jax import lax
from jax.experimental import pallas as pl
from jax.experimental.pallas import tpu as pltpu
from jax.sharding import PartitionSpec as P

MESH = pl.DeviceIdType.MESH
bf, f32 = jnp.bfloat16, jnp.float32

RING = 4
SLOTS = 8
LAG_ONE, LAG_TWO, LAG_THREE = 2, 2, 2
WAIT_ONE, WAIT_TWO, WAIT_THREE = 4.0, 3.5, 3.0
SEND, PASS, SPLIT = (0, 2, 4), (5, 9, 11), (6, 10, 12)
WAIT_GATHER, WAIT_SCATTER, AHEAD = 2.5, 4.0, 0.5


def halves(value):
    high = value.astype(bf)
    return high, (value - high.astype(f32)).astype(bf)


def dot(a, b):
    return jnp.dot(a, b, preferred_element_type=f32)


def kernel(
    a_ref, h_ref, e_ref, o_ref,
    mats, ext, xh, xl, both, first, part, swap,
    in1, sum1, in2, sum2, in3, total,
    near, near_b, terms, in_t, new, new_b, exc, came, came_b,
    s_mat, s_loc, s_carry, r_carry, s_near, r_near, s_fwd, r_fwd,
    s_swap, r_swap, s1, r1, s2, r2, s3, r3, s_t, r_t, s_g, r_g, s_o, r_o,
):
    lag, col = lax.axis_index("lag"), lax.axis_index("col")
    y, k = lag // 2, lag % 2
    z, x = col // RING, col % RING
    pos = {"x": x, "y": y, "z": z}
    other = 1 - k

    def device(**moved):
        at = {**pos, "k": k, **moved}
        return (at["y"] * 2 + at["k"], at["z"] * RING + at["x"])

    def turned(axis, steps):
        return lax.rem(pos[axis] + steps, RING)

    def send(src, dst, s_sem, r_sem, target):
        pltpu.make_async_remote_copy(
            src_ref=src, dst_ref=dst, send_sem=s_sem, recv_sem=r_sem,
            device_id=target, device_id_type=MESH,
        ).start()

    def await_bytes(ref, sem):
        pltpu.make_async_copy(ref, ref, sem).wait()

    load_h = pltpu.make_async_copy(h_ref, ext.at[pl.ds(3, 16)], s_loc.at[0])
    load_h.start()

    barrier = pltpu.get_barrier_semaphore()
    cross = (lax.rem(y + jnp.where(k == 1, 1, RING - 1), RING) * 2 + other, col)
    peers = [device(k=other), cross]
    peers += [device(y=turned("y", d)) for d in range(1, RING)]
    peers += [
        device(z=turned("z", dz), x=turned("x", dx))
        for dz in range(RING) for dx in range(RING) if dz or dx
    ]
    for peer in peers:
        pl.semaphore_signal(barrier, inc=1, device_id=peer, device_id_type=MESH)

    for t in range(4):
        pltpu.make_async_copy(a_ref.at[:, :, :, pl.ds(8 * t, 8)], mats.at[t], s_mat.at[t]).start()
    load_e = pltpu.make_async_copy(e_ref, exc, s_loc.at[1])
    load_e.start()

    ext[0:3] = jnp.zeros((3, 128, 256), f32)
    load_h.wait()

    def set_block(kind, u):
        def piece(i, carry):
            part_rows = pl.ds(pl.multiple_of(32 * i, 32), 32)
            base = ext[1 + 2 * u, part_rows]
            if kind == 0:
                value = base
            else:
                value = ext[(2 + 2 * u) if kind == 1 else 2 * u, part_rows] - base
            rows = pl.ds(pl.multiple_of(u * 128 + 32 * i, 32), 32)
            xh[kind, rows], xl[kind, rows] = halves(value)
            return carry

        lax.fori_loop(0, 4, piece, 0)

    def set_blocks(u, carry):
        for kind in range(3):
            set_block(kind, u)
        return carry

    lax.fori_loop(1, 9, set_blocks, 0)

    def greet():
        pl.semaphore_wait(barrier, len(peers))

        @pl.when(lag < 7)
        def _():
            after = (lag + 1, col)
            send(h_ref.at[15], came.at[2], s_carry.at[0], r_carry.at[0], after)
            send(h_ref.at[pl.ds(13, 2)], came.at[pl.ds(0, 2)], s_carry.at[1], r_carry.at[1], after)

        @pl.when(lag == 0)
        def _():
            came[...] = jnp.zeros((3, 128, 256), f32)
            pltpu.make_async_copy(a_ref.at[pl.ds(0, 3), :, 0], near, s_loc.at[2]).start()

    def near_send(j):
        @pl.when(lag == 0)
        def _():
            for d in (1, 3, 2):
                send(a_ref.at[j, :, d], near.at[j], s_near, r_near.at[j], device(y=d))

    orders = ("xzy", "zxy")

    def scatter(s, n, stage, size, src, dst, s_sem, r_sem):
        axis = orders[n][stage]
        for d in (2, 1, 3):
            to = turned(axis, d)
            send(src.at[pl.ds(to * size, size)], dst.at[d - 1], s_sem, r_sem, device(**{axis: to}))

    def swap_send(s):
        send(part.at[s, other], swap.at[s], s_swap, r_swap.at[s], device(k=other))

    def exchange(s):
        await_bytes(swap.at[s], r_swap.at[s])
        for n in range(2):
            part[s, k, n] += swap[s, n]
        for n in range(2):
            scatter(s, n, 0, 16, part.at[s, k, n], in1.at[s, n], s1, r1.at[s])

    def own(s, n, stage, size):
        return pl.ds(pos[orders[n][stage]] * size, size)

    def one(s):
        await_bytes(in1.at[s], r1.at[s])
        for n in range(2):
            sum1[s, n] = (part[s, k, n, own(s, n, 0, 16)] + in1[s, n, 0]) + (in1[s, n, 1] + in1[s, n, 2])
        for n in range(2):
            scatter(s, n, 1, 4, sum1.at[s, n], in2.at[s, n], s2, r2.at[s])

    def two(s):
        await_bytes(in2.at[s], r2.at[s])
        for n in range(2):
            sum2[s, n] = (sum1[s, n, own(s, n, 1, 4)] + in2[s, n, 0]) + (in2[s, n, 1] + in2[s, n, 2])
        for n in range(2):
            scatter(s, n, 2, 1, sum2.at[s, n], in3.at[s, n], s3, r3.at[s])

    def three(s):
        await_bytes(in3.at[s], r3.at[s])
        for n in range(2):
            value = (sum2[s, n, own(s, n, 2, 1)] + in3[s, n, 0]) + (in3[s, n, 1] + in3[s, n, 2])
            total[2 * (s // 4) + n, lax.rem(s, 4)] = value[0]

    def near_pass(j):
        @pl.when(k == 0)
        def _():
            if j == 0:
                @pl.when(y == 0)
                def _():
                    await_bytes(near, s_loc.at[2])

            @pl.when(y > 0)
            def _():
                await_bytes(near.at[j], r_near.at[j])

            send(near.at[j], near.at[j], s_fwd, r_fwd.at[j], device(k=1))

    def near_split(j):
        @pl.when(k == 1)
        def _():
            await_bytes(near.at[j], r_fwd.at[j])

        def piece(i, carry):
            rows = pl.ds(pl.multiple_of(32 * i, 32), 32)
            high, low = halves(near[j, i])
            near_b[j, rows, 0:128] = high
            near_b[j, rows, 128:256] = high
            near_b[j, rows, 256:384] = low
            return carry

        lax.fori_loop(0, 16, piece, 0)

    def finish(n):
        if n == 0:
            load_e.wait()
        value = exc[n, pl.ds(y * 32, 32), pl.ds(pl.multiple_of(k * 128, 128), 128)] - total[n].reshape(32, 128)
        if n > 0:
            await_bytes(in_t.at[n - 1], r_t.at[n - 1])
            value = value - (terms[n - 1, z, x] + in_t[n - 1].sum(axis=0))
        new[n, y] = value
        for d in (2, 1, 3):
            send(new.at[n, y], new.at[n, y], s_g.at[n], r_g.at[n], device(y=turned("y", d)))

    def add_term(m, n):
        term = dot(near_b[m - n], new_b[n])
        if n > 0:
            term = term + terms[m].reshape(512, 128)
        terms[m] = term.reshape(RING, RING, 32, 128)

    def gathered(n):
        await_bytes(new.at[n, pl.ds(0, 3)], r_g.at[n])
        own = pl.ds(pl.multiple_of(k * 128, 128), 128)
        if n < 3:
            high, low = halves(new[n].reshape(128, 128))
            new_b[n, 0:128] = high
            new_b[n, 128:256] = low
            new_b[n, 256:384] = high
            add_term(n, n)
            for dz in (2, 1, 3, 0):
                for dx in (2, 1, 3, 0):
                    if dz or dx:
                        tz, tx = turned("z", dz), turned("x", dx)
                        send(
                            terms.at[n, tz, tx], in_t.at[n, RING * dz + dx - 1],
                            s_t.at[n], r_t.at[n], device(z=tz, x=tx),
                        )
        o_ref[n, :, own] = new[n].reshape(128, 128)
        send(o_ref.at[n, :, own], o_ref.at[n, :, own], s_o.at[n], r_o.at[n], device(k=other))

    def ahead(n):
        for m in range(n + 1, 3):
            add_term(m, n)

    def build(t):
        for i in range(0, 64, 2):
            top, low = pl.ds(8 * i, 16), pl.ds(512 + 8 * i, 16)
            pair_of = (i // RING, pl.ds(i % RING, 2))
            for u in range(8):
                columns = pl.ds(u * 128, 128)
                even = mats[(t, 2 * u, *pair_of)].reshape(16, 128)
                odd = mats[(t, 2 * u + 1, *pair_of)].reshape(16, 128)
                both[0, top, columns], both[0, low, columns] = halves(even + odd)
                both[1, top, columns], both[1, low, columns] = halves(odd)
                both[2, top, columns], both[2, low, columns] = halves(even)

    def product(kind, pair):
        depth = pl.ds(pl.multiple_of((1 - pair) * 128, 128), 1024)
        stacked = dot(both[kind], xh[kind, depth])
        return stacked[:512] + stacked[512:] + dot(both[kind, 0:512], xl[kind, depth])

    def store(s, n, value, add=False):
        step_x, step_y, step_z = ((16, 1, 4), (4, 1, 16))[n]
        for unit in range(64):
            to = (unit // 16) * step_z + (unit // 4 % 4) * step_x + (unit % 4) * step_y
            for half in range(2):
                piece = value[8 * unit : 8 * unit + 8, half * 128 : half * 128 + 128]
                if add:
                    piece = piece + part[s, half, n, to]
                part[s, half, n, to] = piece

    def late(s):
        for i in range(0, 64, 2):
            high, low = halves(mats[s, 0, i // RING, pl.ds(i % RING, 2)].reshape(16, 128))
            rows = pl.ds(8 * i, 16)
            first[rows, 0:128] = high
            first[rows, 128:256] = high
            first[rows, 256:384] = low
        store(s, 1, dot(first[...], came_b[...]), True)

    def first_came():
        @pl.when(lag > 0)
        def _():
            await_bytes(came.at[2], r_carry.at[0])

        high, low = halves(came[2])
        came_b[0:128] = high
        came_b[128:256] = low
        came_b[256:384] = high
        ext[2] = came[2]
        set_block(2, 1)
        for s in range(2):
            late(s)
            swap_send(s)

    def rest_came():
        @pl.when(lag > 0)
        def _():
            await_bytes(came.at[pl.ds(0, 2)], r_carry.at[1])

        ext[0:2] = came[0:2]
        for kind in range(3):
            set_block(kind, 0)

    acts = ((exchange, 1), (one, 1 + LAG_ONE), (two, 1 + LAG_ONE + LAG_TWO), (three, 1 + LAG_ONE + LAG_TWO + LAG_THREE))

    def when(s, value, act, *args):
        pl.when(s == value)(lambda: act(*args))

    def slot(s, carry):
        pair, t = s // 4, lax.rem(s, 4)

        @pl.when(pair == 0)
        def _():
            await_bytes(mats.at[t], s_mat.at[t])

        build(t)
        base = product(0, pair)
        store(s, 0, base + product(1, pair))
        store(s, 1, base + product(2, pair))
        when(s, 0, greet)
        when(s, 1, first_came)
        pl.when(s > 1)(lambda: swap_send(s))
        when(s, 2, exchange, 0)
        for act, lag_ in acts[::-1]:
            pl.when(s >= lag_ + (act is exchange))(lambda act=act, lag_=lag_: act(s - lag_))
        when(s, 3, rest_came)
        for j in range(3):
            when(s, SEND[j], near_send, j)
            when(s, PASS[j], near_pass, j)
            when(s, SPLIT[j], near_split, j)
        return carry

    lax.fori_loop(0, SLOTS, slot, 0)

    left = []
    for s in range(SLOTS):
        done = 0.0
        for (act, lag_), wait in zip(acts, (1.5, WAIT_ONE, WAIT_TWO, WAIT_THREE)):
            if s + lag_ < SLOTS:
                done = 3.5 * (s + lag_ - SLOTS + 1)
            else:
                done = max(done + wait, 0.1 + 0.01 * s)
                left.append((done, act, s))
                if act is three and s == 3:
                    begin = done
    begin = 0.05 if 3 + acts[-1][1] < SLOTS else begin + 0.001
    time = begin
    for n in range(4):
        left.append((time, finish, n))
        time += WAIT_GATHER
        left.append((time, gathered, n))
        time += WAIT_SCATTER
        if n < 2:
            left.append((time + AHEAD, ahead, n))
    for j in range(3):
        for times, act in ((PASS, near_pass), (SPLIT, near_split)):
            if times[j] >= SLOTS:
                left.append((times[j] - SLOTS + 0.001, act, j))
    for _, act, value in sorted(left, key=lambda item: item[0]):
        act(value)

    for n in range(4):
        await_bytes(o_ref.at[n, :, pl.ds(0, 128)], r_o.at[n])
        await_bytes(o_ref.at[n, :, pl.ds(0, 128)], s_o.at[n])
        await_bytes(new.at[n, pl.ds(0, 3)], s_g.at[n])
    for n in range(3):
        await_bytes(in_t.at[n], s_t.at[n])
    await_bytes(swap, s_swap)
    await_bytes(in1, s1)
    await_bytes(in2, s2)
    await_bytes(in3, s3)

    @pl.when(lag < 7)
    def _():
        await_bytes(came.at[2], s_carry.at[0])
        await_bytes(came.at[pl.ds(0, 2)], s_carry.at[1])

    @pl.when(lag == 0)
    def _():
        for _i in range(3):
            await_bytes(near, s_near)

    @pl.when(k == 0)
    def _():
        await_bytes(near, s_fwd)


def local(lag_matrices, history, excitation):
    DMA = pltpu.SemaphoreType.DMA
    return pl.pallas_call(
        kernel,
        out_shape=jax.ShapeDtypeStruct((4, 128, 256), f32),
        in_specs=[pl.BlockSpec(memory_space=pl.ANY)] * 3,
        out_specs=pl.BlockSpec(memory_space=pltpu.VMEM),
        scratch_shapes=[
            pltpu.VMEM((4, 16, 16, 4, 8, 128), f32),
            pltpu.VMEM((19, 128, 256), f32),
            pltpu.VMEM((3, 1152, 256), bf),
            pltpu.VMEM((3, 1152, 256), bf),
            pltpu.VMEM((3, 1024, 1024), bf),
            pltpu.VMEM((512, 384), bf),
            pltpu.VMEM((SLOTS, 2, 2, 64, 8, 128), f32),
            pltpu.VMEM((SLOTS, 2, 64, 8, 128), f32),
            pltpu.VMEM((SLOTS, 2, 3, 16, 8, 128), f32),
            pltpu.VMEM((SLOTS, 2, 16, 8, 128), f32),
            pltpu.VMEM((SLOTS, 2, 3, 4, 8, 128), f32),
            pltpu.VMEM((SLOTS, 2, 4, 8, 128), f32),
            pltpu.VMEM((SLOTS, 2, 3, 1, 8, 128), f32),
            pltpu.VMEM((4, 4, 8, 128), f32),
            pltpu.VMEM((3, 16, 32, 128), f32),
            pltpu.VMEM((3, 512, 384), bf),
            pltpu.VMEM((3, 4, 4, 32, 128), f32),
            pltpu.VMEM((3, 15, 32, 128), f32),
            pltpu.VMEM((4, 4, 32, 128), f32),
            pltpu.VMEM((3, 384, 128), bf),
            pltpu.VMEM((4, 128, 256), f32),
            pltpu.VMEM((3, 128, 256), f32),
            pltpu.VMEM((384, 256), bf),
            DMA((4,)), DMA((3,)), DMA((2,)), DMA((2,)), DMA, DMA((3,)), DMA, DMA((3,)),
            DMA, DMA((SLOTS,)), DMA, DMA((SLOTS,)), DMA, DMA((SLOTS,)), DMA, DMA((SLOTS,)),
            DMA((3,)), DMA((3,)), DMA((4,)), DMA((4,)), DMA((4,)), DMA((4,)),
        ],
        compiler_params=pltpu.CompilerParams(
            collective_id=0, has_side_effects=True, vmem_limit_bytes=66_000_000
        ),
    )(lag_matrices.reshape(16, 16, 4, 32, 128), history, excitation)


def solution(mesh):
    return jax.shard_map(
        local,
        mesh=mesh,
        in_specs=(P("lag", None, "col"), P("lag", "col", None), P(None, "col", None)),
        out_specs=P(None, "col", None),
        check_vma=False,
    )
```

```python
import jax
import jax.numpy as jnp
from jax import lax
from jax.experimental import pallas as pl
from jax.experimental.pallas import tpu as pltpu
from jax.sharding import PartitionSpec as P

MESH = pl.DeviceIdType.MESH
bf, f32 = jnp.bfloat16, jnp.float32

RING = 4
SLOTS = 8
LAG_ONE, LAG_TWO, LAG_THREE = 2, 2, 2
WAIT_ONE, WAIT_TWO, WAIT_THREE = 4.0, 3.5, 3.0
SEND, PASS, SPLIT = (0, 2, 4), (5, 9, 11), (6, 10, 12)
WAIT_GATHER, WAIT_SCATTER, AHEAD = 2.5, 4.0, 0.5


def halves(value):
    high = value.astype(bf)
    return high, (value - high.astype(f32)).astype(bf)


def dot(a, b):
    return jnp.dot(a, b, preferred_element_type=f32)


def kernel(
    a_ref, h_ref, e_ref, o_ref,
    mats, ext, xh, xl, both, first, part, swap,
    in1, sum1, in2, sum2, in3, total,
    near, near_b, terms, in_t, new, new_b, exc, came, came_b,
    s_mat, s_loc, s_carry, r_carry, s_near, r_near, s_fwd, r_fwd,
    s_swap, r_swap, s1, r1, s2, r2, s3, r3, s_t, r_t, s_g, r_g, s_o, r_o,
):
    lag, col = lax.axis_index("lag"), lax.axis_index("col")
    y, k = lag // 2, lag % 2
    z, x = col // RING, col % RING
    pos = {"x": x, "y": y, "z": z}
    other = 1 - k

    def device(**moved):
        at = {**pos, "k": k, **moved}
        return (at["y"] * 2 + at["k"], at["z"] * RING + at["x"])

    def turned(axis, steps):
        return lax.rem(pos[axis] + steps, RING)

    def send(src, dst, s_sem, r_sem, target):
        pltpu.make_async_remote_copy(
            src_ref=src, dst_ref=dst, send_sem=s_sem, recv_sem=r_sem,
            device_id=target, device_id_type=MESH,
        ).start()

    def await_bytes(ref, sem):
        pltpu.make_async_copy(ref, ref, sem).wait()

    load_h = pltpu.make_async_copy(h_ref, ext.at[pl.ds(3, 16)], s_loc.at[0])
    load_h.start()

    barrier = pltpu.get_barrier_semaphore()
    cross = (lax.rem(y + jnp.where(k == 1, 1, RING - 1), RING) * 2 + other, col)
    peers = [device(k=other), cross]
    peers += [device(y=turned("y", d)) for d in range(1, RING)]
    peers += [
        device(z=turned("z", dz), x=turned("x", dx))
        for dz in range(RING) for dx in range(RING) if dz or dx
    ]
    for peer in peers:
        pl.semaphore_signal(barrier, inc=1, device_id=peer, device_id_type=MESH)

    for t in range(4):
        pltpu.make_async_copy(a_ref.at[:, :, :, pl.ds(8 * t, 8)], mats.at[t], s_mat.at[t]).start()
    load_e = pltpu.make_async_copy(e_ref, exc, s_loc.at[1])
    load_e.start()

    ext[0:3] = jnp.zeros((3, 128, 256), f32)
    load_h.wait()

    def set_block(kind, u):
        def piece(i, carry):
            part_rows = pl.ds(pl.multiple_of(32 * i, 32), 32)
            base = ext[1 + 2 * u, part_rows]
            if kind == 0:
                value = base
            else:
                value = ext[(2 + 2 * u) if kind == 1 else 2 * u, part_rows] - base
            rows = pl.ds(pl.multiple_of(u * 128 + 32 * i, 32), 32)
            xh[kind, rows], xl[kind, rows] = halves(value)
            return carry

        lax.fori_loop(0, 4, piece, 0)

    def set_blocks(u, carry):
        for kind in range(3):
            set_block(kind, u)
        return carry

    lax.fori_loop(1, 9, set_blocks, 0)

    def greet():
        pl.semaphore_wait(barrier, len(peers))

        @pl.when(lag < 7)
        def _():
            after = (lag + 1, col)
            send(h_ref.at[15], came.at[2], s_carry.at[0], r_carry.at[0], after)
            send(h_ref.at[pl.ds(13, 2)], came.at[pl.ds(0, 2)], s_carry.at[1], r_carry.at[1], after)

        @pl.when(lag == 0)
        def _():
            came[...] = jnp.zeros((3, 128, 256), f32)
            pltpu.make_async_copy(a_ref.at[pl.ds(0, 3), :, 0], near, s_loc.at[2]).start()

    def near_send(j):
        @pl.when(lag == 0)
        def _():
            for d in (1, 3, 2):
                send(a_ref.at[j, :, d], near.at[j], s_near, r_near.at[j], device(y=d))

    orders = ("xzy", "zxy")

    def scatter(s, n, stage, size, src, dst, s_sem, r_sem):
        axis = orders[n][stage]
        for d in (2, 1, 3):
            to = turned(axis, d)
            send(src.at[pl.ds(to * size, size)], dst.at[d - 1], s_sem, r_sem, device(**{axis: to}))

    def swap_send(s):
        send(part.at[s, other], swap.at[s], s_swap, r_swap.at[s], device(k=other))

    def exchange(s):
        await_bytes(swap.at[s], r_swap.at[s])
        for n in range(2):
            part[s, k, n] += swap[s, n]
        for n in range(2):
            scatter(s, n, 0, 16, part.at[s, k, n], in1.at[s, n], s1, r1.at[s])

    def own(s, n, stage, size):
        return pl.ds(pos[orders[n][stage]] * size, size)

    def one(s):
        await_bytes(in1.at[s], r1.at[s])
        for n in range(2):
            sum1[s, n] = (part[s, k, n, own(s, n, 0, 16)] + in1[s, n, 0]) + (in1[s, n, 1] + in1[s, n, 2])
        for n in range(2):
            scatter(s, n, 1, 4, sum1.at[s, n], in2.at[s, n], s2, r2.at[s])

    def two(s):
        await_bytes(in2.at[s], r2.at[s])
        for n in range(2):
            sum2[s, n] = (sum1[s, n, own(s, n, 1, 4)] + in2[s, n, 0]) + (in2[s, n, 1] + in2[s, n, 2])
        for n in range(2):
            scatter(s, n, 2, 1, sum2.at[s, n], in3.at[s, n], s3, r3.at[s])

    def three(s):
        await_bytes(in3.at[s], r3.at[s])
        for n in range(2):
            value = (sum2[s, n, own(s, n, 2, 1)] + in3[s, n, 0]) + (in3[s, n, 1] + in3[s, n, 2])
            total[2 * (s // 4) + n, lax.rem(s, 4)] = value[0]

    def near_pass(j):
        @pl.when(k == 0)
        def _():
            if j == 0:
                @pl.when(y == 0)
                def _():
                    await_bytes(near, s_loc.at[2])

            @pl.when(y > 0)
            def _():
                await_bytes(near.at[j], r_near.at[j])

            send(near.at[j], near.at[j], s_fwd, r_fwd.at[j], device(k=1))

    def near_split(j):
        @pl.when(k == 1)
        def _():
            await_bytes(near.at[j], r_fwd.at[j])

        def piece(i, carry):
            rows = pl.ds(pl.multiple_of(32 * i, 32), 32)
            high, low = halves(near[j, i])
            near_b[j, rows, 0:128] = high
            near_b[j, rows, 128:256] = high
            near_b[j, rows, 256:384] = low
            return carry

        lax.fori_loop(0, 16, piece, 0)

    def finish(n):
        if n == 0:
            load_e.wait()
        value = exc[n, pl.ds(y * 32, 32), pl.ds(pl.multiple_of(k * 128, 128), 128)] - total[n].reshape(32, 128)
        if n > 0:
            await_bytes(in_t.at[n - 1], r_t.at[n - 1])
            value = value - (terms[n - 1, z, x] + in_t[n - 1].sum(axis=0))
        new[n, y] = value
        for d in (2, 1, 3):
            send(new.at[n, y], new.at[n, y], s_g.at[n], r_g.at[n], device(y=turned("y", d)))

    def add_term(m, n):
        term = dot(near_b[m - n], new_b[n])
        if n > 0:
            term = term + terms[m].reshape(512, 128)
        terms[m] = term.reshape(RING, RING, 32, 128)

    def gathered(n):
        await_bytes(new.at[n, pl.ds(0, 3)], r_g.at[n])
        own = pl.ds(pl.multiple_of(k * 128, 128), 128)
        if n < 3:
            high, low = halves(new[n].reshape(128, 128))
            new_b[n, 0:128] = high
            new_b[n, 128:256] = low
            new_b[n, 256:384] = high
            add_term(n, n)
            for dz in (2, 1, 3, 0):
                for dx in (2, 1, 3, 0):
                    if dz or dx:
                        tz, tx = turned("z", dz), turned("x", dx)
                        send(
                            terms.at[n, tz, tx], in_t.at[n, RING * dz + dx - 1],
                            s_t.at[n], r_t.at[n], device(z=tz, x=tx),
                        )
        o_ref[n, :, own] = new[n].reshape(128, 128)
        send(o_ref.at[n, :, own], o_ref.at[n, :, own], s_o.at[n], r_o.at[n], device(k=other))

    def ahead(n):
        for m in range(n + 1, 3):
            add_term(m, n)

    def build(t):
        for i in range(0, 64, 2):
            top, low = pl.ds(8 * i, 16), pl.ds(512 + 8 * i, 16)
            pair_of = (i // RING, pl.ds(i % RING, 2))
            for u in range(8):
                columns = pl.ds(u * 128, 128)
                even = mats[(t, 2 * u, *pair_of)].reshape(16, 128)
                odd = mats[(t, 2 * u + 1, *pair_of)].reshape(16, 128)
                both[0, top, columns], both[0, low, columns] = halves(even + odd)
                both[1, top, columns], both[1, low, columns] = halves(odd)
                both[2, top, columns], both[2, low, columns] = halves(even)

    def product(kind, pair):
        depth = pl.ds(pl.multiple_of((1 - pair) * 128, 128), 1024)
        stacked = dot(both[kind], xh[kind, depth])
        return stacked[:512] + stacked[512:] + dot(both[kind, 0:512], xl[kind, depth])

    def store(s, n, value, add=False):
        step_x, step_y, step_z = ((16, 1, 4), (4, 1, 16))[n]
        for unit in range(64):
            to = (unit // 16) * step_z + (unit // 4 % 4) * step_x + (unit % 4) * step_y
            for half in range(2):
                piece = value[8 * unit : 8 * unit + 8, half * 128 : half * 128 + 128]
                if add:
                    piece = piece + part[s, half, n, to]
                part[s, half, n, to] = piece

    def late(s):
        for i in range(0, 64, 2):
            high, low = halves(mats[s, 0, i // RING, pl.ds(i % RING, 2)].reshape(16, 128))
            rows = pl.ds(8 * i, 16)
            first[rows, 0:128] = high
            first[rows, 128:256] = high
            first[rows, 256:384] = low
        store(s, 1, dot(first[...], came_b[...]), True)

    def first_came():
        @pl.when(lag > 0)
        def _():
            await_bytes(came.at[2], r_carry.at[0])

        high, low = halves(came[2])
        came_b[0:128] = high
        came_b[128:256] = low
        came_b[256:384] = high
        ext[2] = came[2]
        set_block(2, 1)
        late(0)
        swap_send(0)

    def rest_came():
        @pl.when(lag > 0)
        def _():
            await_bytes(came.at[pl.ds(0, 2)], r_carry.at[1])

        ext[0:2] = came[0:2]
        for kind in range(3):
            set_block(kind, 0)

    acts = ((exchange, 1), (one, 1 + LAG_ONE), (two, 1 + LAG_ONE + LAG_TWO), (three, 1 + LAG_ONE + LAG_TWO + LAG_THREE))

    def when(s, value, act, *args):
        pl.when(s == value)(lambda: act(*args))

    def slot(s, carry):
        pair, t = s // 4, lax.rem(s, 4)

        @pl.when(pair == 0)
        def _():
            await_bytes(mats.at[t], s_mat.at[t])

        build(t)
        base = product(0, pair)
        store(s, 0, base + product(1, pair))
        store(s, 1, base + product(2, pair))
        when(s, 0, first_came)
        pl.when(s > 0)(lambda: swap_send(s))
        for act, lag_ in acts[::-1]:
            pl.when(s >= lag_)(lambda act=act, lag_=lag_: act(s - lag_))
        when(s, 3, rest_came)
        for j in range(3):
            when(s, SEND[j], near_send, j)
            when(s, PASS[j], near_pass, j)
            when(s, SPLIT[j], near_split, j)
        return carry

    greet()
    lax.fori_loop(0, SLOTS, slot, 0)

    left = []
    for s in range(SLOTS):
        done = 0.0
        for (act, lag_), wait in zip(acts, (1.5, WAIT_ONE, WAIT_TWO, WAIT_THREE)):
            if s + lag_ < SLOTS:
                done = 3.5 * (s + lag_ - SLOTS + 1)
            else:
                done = max(done + wait, 0.1 + 0.01 * s)
                left.append((done, act, s))
                if act is three and s == 3:
                    begin = done
    begin = 0.05 if 3 + acts[-1][1] < SLOTS else begin + 0.001
    time = begin
    for n in range(4):
        left.append((time, finish, n))
        time += WAIT_GATHER
        left.append((time, gathered, n))
        time += WAIT_SCATTER
        if n < 2:
            left.append((time + AHEAD, ahead, n))
    for j in range(3):
        for times, act in ((PASS, near_pass), (SPLIT, near_split)):
            if times[j] >= SLOTS:
                left.append((times[j] - SLOTS + 0.001, act, j))
    for _, act, value in sorted(left, key=lambda item: item[0]):
        act(value)

    for n in range(4):
        await_bytes(o_ref.at[n, :, pl.ds(0, 128)], r_o.at[n])
        await_bytes(o_ref.at[n, :, pl.ds(0, 128)], s_o.at[n])
        await_bytes(new.at[n, pl.ds(0, 3)], s_g.at[n])
    for n in range(3):
        await_bytes(in_t.at[n], s_t.at[n])
    await_bytes(swap, s_swap)
    await_bytes(in1, s1)
    await_bytes(in2, s2)
    await_bytes(in3, s3)

    @pl.when(lag < 7)
    def _():
        await_bytes(came.at[2], s_carry.at[0])
        await_bytes(came.at[pl.ds(0, 2)], s_carry.at[1])

    @pl.when(lag == 0)
    def _():
        for _i in range(3):
            await_bytes(near, s_near)

    @pl.when(k == 0)
    def _():
        await_bytes(near, s_fwd)


def local(lag_matrices, history, excitation):
    DMA = pltpu.SemaphoreType.DMA
    return pl.pallas_call(
        kernel,
        out_shape=jax.ShapeDtypeStruct((4, 128, 256), f32),
        in_specs=[pl.BlockSpec(memory_space=pl.ANY)] * 3,
        out_specs=pl.BlockSpec(memory_space=pltpu.VMEM),
        scratch_shapes=[
            pltpu.VMEM((4, 16, 16, 4, 8, 128), f32),
            pltpu.VMEM((19, 128, 256), f32),
            pltpu.VMEM((3, 1152, 256), bf),
            pltpu.VMEM((3, 1152, 256), bf),
            pltpu.VMEM((3, 1024, 1024), bf),
            pltpu.VMEM((512, 384), bf),
            pltpu.VMEM((SLOTS, 2, 2, 64, 8, 128), f32),
            pltpu.VMEM((SLOTS, 2, 64, 8, 128), f32),
            pltpu.VMEM((SLOTS, 2, 3, 16, 8, 128), f32),
            pltpu.VMEM((SLOTS, 2, 16, 8, 128), f32),
            pltpu.VMEM((SLOTS, 2, 3, 4, 8, 128), f32),
            pltpu.VMEM((SLOTS, 2, 4, 8, 128), f32),
            pltpu.VMEM((SLOTS, 2, 3, 1, 8, 128), f32),
            pltpu.VMEM((4, 4, 8, 128), f32),
            pltpu.VMEM((3, 16, 32, 128), f32),
            pltpu.VMEM((3, 512, 384), bf),
            pltpu.VMEM((3, 4, 4, 32, 128), f32),
            pltpu.VMEM((3, 15, 32, 128), f32),
            pltpu.VMEM((4, 4, 32, 128), f32),
            pltpu.VMEM((3, 384, 128), bf),
            pltpu.VMEM((4, 128, 256), f32),
            pltpu.VMEM((3, 128, 256), f32),
            pltpu.VMEM((384, 256), bf),
            DMA((4,)), DMA((3,)), DMA((2,)), DMA((2,)), DMA, DMA((3,)), DMA, DMA((3,)),
            DMA, DMA((SLOTS,)), DMA, DMA((SLOTS,)), DMA, DMA((SLOTS,)), DMA, DMA((SLOTS,)),
            DMA((3,)), DMA((3,)), DMA((4,)), DMA((4,)), DMA((4,)), DMA((4,)),
        ],
        compiler_params=pltpu.CompilerParams(
            collective_id=0, has_side_effects=True, vmem_limit_bytes=66_000_000
        ),
    )(lag_matrices.reshape(16, 16, 4, 32, 128), history, excitation)


def solution(mesh):
    return jax.shard_map(
        local,
        mesh=mesh,
        in_specs=(P("lag", None, "col"), P("lag", "col", None), P(None, "col", None)),
        out_specs=P(None, "col", None),
        check_vma=False,
    )
```
